128 devices in a mesh: spec: 16 (over y, z), led: 8 (over x, core).
Axes of the slice: x: 4, y: 4, z: 4, core: 2. Of those that a mesh axis runs over, the one named last changes fastest.
Arguments:
- spectrum: float32 [16, 2, 2048, 256], P('spec'), may hold values from -6 to 6
- images: float32 [16, 2, 1024, 1024], P('spec', None, 'led'), may hold values from -6 to 6
- zernike: float32 [16, 16], P('spec'), may hold values from -6 to 6
- pupil_modes: float32 [16, 4, 31], P('led'), may hold values from -0.1875 to 0.1875
- patch_tiles: int32 [16, 25], replicated, may hold values from 0 to 127, as said below
- patch_offsets: int32 [16, 2], replicated, may hold values from 0 to 226
Outputs:
- new_spectrum: float32 [16, 2, 2048, 256], P('spec')
- solve_residual: float32 [16, 2, 2048, 256], P('spec')
The draws below stay inside these ranges and needn't reach their ends.
Inputs may be any that keep to these rules, and one draw needn't show every extreme that they name: Row l of patch_tiles lists the ids (r + i) * 16 + c + j of a block of 5 x 5 tiles with top left tile (r, c), i and j from 0 to 4, row by row.
All inputs are finite; a program needn't handle non-finite values.
Results may differ from the reference program's by a relative error of at most 0.0003.
Values sent between devices are 32-bit elements; how exact they have to be, the bound alone decides.
No kernel may reach another device: no remote copies, remote signals or barrier semaphores. Data moves between devices by JAX's collectives and lax.ppermute only.
A program may use at most 192 MiB of HBM per device.

```python
import jax
import jax.numpy as jnp
from jax import lax

TILE = 256
WIN = 5
TAPS = 31
CHANNELS = 16
IMG = 1024
ITERS = 1
ROWS = 8
COLS = 16
LEDS = 16


def draw_patch_tiles(key, part):
    key_rows, key_cols = jax.random.split(key, 2)
    top_rows = jax.random.randint(key_rows, (LEDS,), 0, ROWS - WIN + 1).astype(jnp.int32)
    left_cols = jax.random.randint(key_cols, (LEDS,), 0, COLS - WIN + 1).astype(jnp.int32)
    top_rows = top_rows.at[0].set(0).at[LEDS - 1].set(ROWS - WIN)
    left_cols = left_cols.at[0].set(0).at[LEDS - 1].set(COLS - WIN)
    row_steps = jnp.arange(WIN, dtype=jnp.int32)[:, None]
    col_steps = jnp.arange(WIN, dtype=jnp.int32)[None, :]
    tile_ids = (top_rows[:, None, None] + row_steps) * COLS + left_cols[:, None, None] + col_steps
    return tile_ids.reshape(LEDS, WIN * WIN).astype(jnp.int32)


def place_ends(result, own_key, low, largest):
    place = [jax.random.randint(jax.random.fold_in(own_key, axis), (), 0, length) for axis, length in enumerate(result.shape)]
    widest = result.shape.index(max(result.shape))
    next_to = place[:widest] + [(place[widest] + 1) % result.shape[widest]] + place[widest + 1:]
    return result.at[tuple(place)].set(low).at[tuple(next_to)].set(largest)


def steps_of(stream_key, shape, pieces, least, largest):
    gain = 1.0
    for position, blocks in pieces:
        heights = jax.random.uniform(jax.random.fold_in(jax.random.fold_in(stream_key, 6), position), (blocks,), jnp.float32, least / len(pieces), largest / len(pieces))
        gain = gain * jnp.repeat(jnp.exp(heights), shape[position] // blocks).reshape((-1,) + (1,) * (len(shape) - 1 - position))
    return gain


def scatter_about(rng, extent, scale, reach, shards=(), held_as=jnp.bfloat16):
    result = jax.random.normal(rng, extent, jnp.float32) * scale
    if len(shards) > 0:
        result = steps_of(rng, extent, shards, -0.22, 0.18) * result
    return jnp.clip(result, min=-reach, max=reach).astype(held_as)


def setup_inputs(seed: int = 0) -> dict:
    key_list = jax.random.split(jax.random.key(seed), 7)
    spectrum = scatter_about(key_list[0], (COLS, 2, ROWS * TILE, TILE), 1.0, 6.0, ((0, 16),), jnp.float32)
    images = scatter_about(key_list[1], (LEDS, 2, IMG, IMG), 1.0, 6.0, ((0, 16), (2, 8)), jnp.float32)
    zernike = scatter_about(key_list[2], (LEDS, CHANNELS), 1.0, 6.0, ((0, 16),), jnp.float32)
    pupil_modes = scatter_about(key_list[3], (CHANNELS, 4, TAPS), (2 * CHANNELS * TAPS) ** -0.5, 0.1875, ((0, 8),), jnp.float32)
    patch_tiles = draw_patch_tiles(jax.random.fold_in(key_list[6], 71), 0)
    patch_offsets = place_ends(jax.random.randint(key_list[5], (LEDS, 2), 0, WIN * TILE - IMG - TAPS + 2), jax.random.fold_in(key_list[5], 1), 0, (WIN * TILE - IMG - TAPS + 2) - 1).astype(jnp.int32)
    return dict(spectrum=spectrum, images=images, zernike=zernike, pupil_modes=pupil_modes, patch_tiles=patch_tiles, patch_offsets=patch_offsets)


damping = 0.5


def toeplitz(kernel, offset, rows_len, cols_len):
    tap_count = kernel.shape[-1]
    distance = jnp.arange(rows_len, dtype=jnp.int32)[:, None] - offset - jnp.arange(cols_len, dtype=jnp.int32)[None, :]
    matrix = jnp.zeros((2, rows_len, cols_len), kernel.dtype)
    for tap in range(tap_count):
        matrix = matrix + jnp.where(distance[None, :, :] == tap, kernel[:, tap][:, None, None], jnp.zeros((), kernel.dtype))
    return matrix


def complex_product(left_side, right_side):
    real_part = jnp.dot(left_side[0], right_side[0], precision=lax.Precision.HIGHEST) - jnp.dot(left_side[1], right_side[1], precision=lax.Precision.HIGHEST)
    imag_part = jnp.dot(left_side[0], right_side[1], precision=lax.Precision.HIGHEST) + jnp.dot(left_side[1], right_side[0], precision=lax.Precision.HIGHEST)
    return jnp.stack([real_part, imag_part])


def plain_swap(matrix):
    return jnp.stack([matrix[0].T, matrix[1].T])


def conj_swap(matrix):
    return jnp.stack([matrix[0].T, -matrix[1].T])


def conjugate(matrix):
    return jnp.stack([matrix[0], -matrix[1]])


def forward_cols(window, col_map):
    return complex_product(window, col_map)


def forward_rows(columns, row_map):
    return complex_product(plain_swap(row_map), columns)


def adjoint_rows(picture, row_map):
    return complex_product(conjugate(row_map), picture)


def adjoint_cols(columns, col_map):
    return complex_product(columns, conj_swap(col_map))


def reference(spectrum, images, zernike, pupil_modes, patch_tiles, patch_offsets):
    block_len = WIN * TILE
    row_cells = ROWS * TILE
    anchor = jnp.int32(0)
    kernels = jnp.dot(zernike, pupil_modes.reshape(CHANNELS, 4 * TAPS), precision=lax.Precision.HIGHEST).reshape(LEDS, 4, TAPS)

    def to_grid(tiles):
        return tiles.transpose(1, 2, 0, 3).reshape(2, row_cells, COLS * TILE)

    def to_tiles(grid):
        return grid.reshape(2, row_cells, COLS, TILE).transpose(2, 0, 1, 3)

    def normal_sweep(source_tiles, with_data):
        source_grid = to_grid(source_tiles)

        def advance(accumulated, member):
            first_tile, offsets, kernel, picture = member
            top_row = (first_tile // COLS) * TILE
            left_col = (first_tile % COLS) * TILE
            col_map = toeplitz(kernel[0:2], offsets[1], block_len, IMG)
            row_map = toeplitz(kernel[2:4], offsets[0], block_len, IMG)
            window = lax.dynamic_slice(source_grid, (anchor, top_row, left_col), (2, block_len, block_len))
            modelled = forward_rows(forward_cols(window, col_map), row_map)
            misfit = picture - modelled if with_data else modelled
            returned = adjoint_cols(adjoint_rows(misfit, row_map), col_map)
            current = lax.dynamic_slice(accumulated, (anchor, top_row, left_col), (2, block_len, block_len))
            return lax.dynamic_update_slice(accumulated, current + returned, (anchor, top_row, left_col)), None

        total = lax.scan(advance, jnp.zeros_like(source_grid), (patch_tiles[:, 0], patch_offsets, kernels, images))[0]
        return to_tiles(total)

    residual = normal_sweep(spectrum, True) - damping * spectrum
    direction = residual
    update = jnp.zeros_like(residual)
    norm_now = jnp.sum(residual * residual)
    for iteration in range(ITERS):
        image_dir = normal_sweep(direction, False) + damping * direction
        step_size = norm_now / jnp.sum(direction * image_dir)
        update = update + step_size * direction
        residual = residual - step_size * image_dir
        norm_next = jnp.sum(residual * residual)
        direction = residual + (norm_next / norm_now) * direction
        norm_now = norm_next
    return spectrum + update, residual
```

```python
import functools

import jax
import jax.numpy as jnp
from jax import lax
from jax.experimental import pallas as pl
from jax.experimental.pallas import tpu as pltpu
from jax.sharding import PartitionSpec as P

WIN = 5
DAMPING = 0.5
HALO = 32
RING = 384
F32 = jnp.float32
BF16 = jnp.bfloat16


def split(value):
    high = value.astype(BF16)
    return high, (value - high.astype(F32)).astype(BF16)


def dot3(left_high, left_low, right_high, right_low):
    left = jnp.concatenate([left_high, left_high, left_low], axis=1)
    right = jnp.concatenate([right_high, right_low, right_high], axis=0)
    return jnp.dot(left, right, preferred_element_type=F32)


def band(row, rows, shift):
    lanes = row.shape[1]
    return pltpu.roll(
        jnp.broadcast_to(row, (rows, lanes)), shift % lanes, 1, stride=1, stride_axis=0
    )


def pack_edges(tile, toward_left):
    lane = lax.broadcasted_iota(jnp.int32, (tile.shape[0], 128), 1)
    if toward_left:
        real, imag, kept = tile[:, 0:128], tile[:, 256:384], lane < HALO
    else:
        real, imag, kept = tile[:, 128:256], tile[:, 384:512], lane >= 128 - HALO
    zero = jnp.zeros_like(real)
    return jnp.where(kept, real, zero) + pltpu.roll(jnp.where(kept, imag, zero), 64, 1)


def slots_kernel(info, picture, out, wide):
    slot = pl.program_id(0)

    @pl.when(slot == 0)
    def _():
        for part in range(2):
            image = picture[0, part]
            blank = jnp.zeros((image.shape[0], wide.shape[2] - image.shape[1]), F32)
            wide[part] = pltpu.roll(jnp.concatenate([image, blank], axis=1), info[1], 1)

    step = slot - info[0]
    inside = (step >= 0) & (step < WIN)

    @pl.when(inside)
    def _():
        start = pl.multiple_of(step * 256, 256)
        out[0] = wide[:, :, pl.ds(start, 256)]

    @pl.when(jnp.logical_not(inside))
    def _():
        out[...] = jnp.zeros_like(out)


def cut_kernel(info, main, below, above, f_main, f_below, f_above, to_left, to_right):
    own = info[0]
    last = info[1]
    body_rows = jnp.concatenate([main[0, 0], main[0, 1]], axis=1)
    under = jnp.concatenate([below[0, 0], below[0, 1]], axis=1)
    over = jnp.concatenate([above[0, 0], above[0, 1]], axis=1)
    under = jnp.where(own < last, under, jnp.zeros_like(under))
    over = jnp.where(own > 0, over, jnp.zeros_like(over))
    f_main[...] = body_rows
    f_below[...] = under
    f_above[...] = over
    start = 0
    for rows in (body_rows, under, over):
        end = start + rows.shape[0]
        to_left[start:end] = pack_edges(rows, True)
        to_right[start:end] = pack_edges(rows, False)
        start = end


def load_field(pieces, left_high, left_low):
    mains = jnp.concatenate([piece[0][...] for piece in pieces], axis=0)
    halos = jnp.concatenate(
        [functools.reduce(lambda a, b: a + b, [h[...] for h in piece[1]]) for piece in pieces],
        axis=0,
    )
    lane = lax.broadcasted_iota(jnp.int32, halos.shape, 1)
    imag_lane = (lane >= HALO) & (lane < 3 * HALO)
    signed = jnp.where(imag_lane, -halos, halos)
    real, imag = mains[:, 0:256], mains[:, 256:512]
    rows = mains.shape[0]
    for start, parts in (
        (0, (real, -imag, signed)),
        (rows, (imag, real, pltpu.roll(halos, 64, 1))),
    ):
        high, low = split(jnp.concatenate(parts, axis=1))
        left_high[start : start + rows] = high
        left_low[start : start + rows] = low


def apply_pair(left_high, left_low, col_high, col_low, row_high, row_low):
    columns = dot3(left_high[...], left_low[...], col_high, col_low)
    rows = columns.shape[0] // 2

    def right_operand(part):
        real, imag = part[0:rows], part[rows:]
        rm, rr, rl = real[0:256], real[256:288], real[288:320]
        im, ir, il = imag[0:256], imag[256:288], imag[288:320]
        to_real = jnp.concatenate([rm, -im, rr, -il, -ir, rl], axis=0)
        to_imag = jnp.concatenate([im, rm, ir, rl, rr, il], axis=0)
        return jnp.concatenate([to_real, to_imag], axis=1)

    high, low = split(columns)
    return dot3(row_high, row_low, right_operand(high), right_operand(low))


def touches(distance, image_len, reach):
    return (distance > -256) & (distance < image_len + reach)


def first_kernel(
    image_len, reach, col_at, row_at, taps, f_main, f_below, f_above, from_left, from_right,
    total, col_high, col_low, row_high, row_low, left_high, left_low,
):
    led = pl.program_id(0)

    @pl.when(led == 0)
    def _():
        total[...] = DAMPING * f_main[...]
        cuts = ((0, 256), (256, 288), (288, 320))
        pieces = [
            (ref, (from_left.at[a:b], from_right.at[a:b]))
            for ref, (a, b) in zip((f_main, f_below, f_above), cuts)
        ]
        load_field(pieces, left_high, left_low)

    at_col, at_row = col_at[led], row_at[led]

    @pl.when(touches(at_col, image_len, reach) & touches(at_row, image_len, reach))
    def _():
        spot = lax.broadcasted_iota(jnp.int32, (RING, 1), 0)
        place = jnp.where(spot < 256, spot, spot - RING)

        def seen(at):
            inside = (place >= -HALO) & (place + at >= 0) & (place + at < image_len)
            return inside.astype(F32)

        def forward_band(which):
            return band(taps[0, which : which + 1], RING, 0)

        def backward_band(which, rows):
            return band(taps[0, 4 + which : 5 + which], rows, -HALO)

        def product(a_real, a_imag, b_real, b_imag, sign):
            upper = jnp.concatenate([a_real, a_imag], axis=1)
            lower = jnp.concatenate([sign * a_imag, -sign * a_real], axis=1)
            left = split(jnp.concatenate([upper, lower], axis=0))
            right = split(jnp.concatenate([b_real, b_imag], axis=0))
            return dot3(*left, *right)

        def without_gap(a):
            return jnp.concatenate([a[0:288], a[352:384]], axis=0)

        mask = seen(at_col)
        gram = product(
            without_gap(backward_band(0, RING)), without_gap(backward_band(1, RING)),
            forward_band(0)[:, 0:256] * mask, forward_band(1)[:, 0:256] * mask, 1.0,
        )
        real, imag = gram[0:320], gram[320:640]
        col_pair = jnp.concatenate(
            [
                real[0:256], imag[0:256],
                real[256:288], imag[288:320], imag[256:288], real[288:320],
            ],
            axis=0,
        )
        high, low = split(col_pair)
        col_high[0] = high
        col_low[0] = low

        mask = seen(at_row)
        gram = product(
            backward_band(2, 256), backward_band(3, 256),
            forward_band(2) * mask, forward_band(3) * mask, -1.0,
        )
        real, imag = gram[0:256], gram[256:512]
        edge = real[:, 256:384] + pltpu.roll(imag[:, 256:384], 64, 1)
        high, low = split(jnp.concatenate([real[:, 0:256], imag[:, 0:256], edge], axis=1))
        row_high[0] = high
        row_low[0] = low
        total[...] += apply_pair(
            left_high, left_low, col_high[0], col_low[0], row_high[0], row_low[0]
        )


def second_kernel(
    image_len, reach, col_at, row_at, col_high, col_low, row_high, row_low,
    r_main, r_below, r_above, ml, mr, bl, br, al, ar,
    total, inner, left_high, left_low,
):
    led = pl.program_id(0)

    @pl.when(led == 0)
    def _():
        total[...] = DAMPING * r_main[...]
        pieces = [(r_main, (ml, mr)), (r_below, (bl, br)), (r_above, (al, ar))]
        load_field(pieces, left_high, left_low)

    @pl.when(touches(col_at[led], image_len, reach) & touches(row_at[led], image_len, reach))
    def _():
        total[...] += apply_pair(
            left_high, left_low, col_high[0], col_low[0], row_high[0], row_low[0]
        )

    @pl.when(led == pl.num_programs(0) - 1)
    def _():
        inner[...] = jnp.broadcast_to(jnp.sum(total[...] * r_main[...]), inner.shape)


def data_kernel(
    image_len, reach, col_at, starts, taps, pieces, out, field, spill
):
    led = pl.program_id(0)

    @pl.when(led == 0)
    def _():
        field[...] = jnp.zeros_like(field)
        spill[...] = jnp.zeros_like(spill)

    @pl.when(touches(col_at[led], image_len, 0))
    def _():
        strip = pieces.shape[2]
        real, imag = pieces[0, 0], pieces[0, 1]
        left = jnp.concatenate(
            [
                jnp.concatenate([real, imag], axis=1),
                jnp.concatenate([imag, -real], axis=1),
            ],
            axis=0,
        )
        right = jnp.concatenate(
            [band(taps[0, 0:1], 256, 0), band(taps[0, 1:2], 256, 0)], axis=0
        )
        wide = dot3(*split(left), *split(right))
        turned = jnp.concatenate([wide[strip:], -wide[0:strip]], axis=0)
        edge = wide[:, 256:384] + pltpu.roll(turned[:, 256:384], 64, 1)
        right = jnp.concatenate([wide[:, 0:256], turned[:, 0:256], edge], axis=1)
        start = starts[led]
        below = lax.rem(start, 8)
        base = pl.multiple_of(start - below, 8)
        tall = strip + 40

        def moved(which):
            matrix = band(taps[0, 4 + which : 5 + which, 0:256], tall, -HALO)[:, 0:strip]
            return pltpu.roll(matrix, below, 0)

        left = jnp.concatenate([moved(2), moved(3)], axis=1)
        added = dot3(*split(left), *split(right))
        field[pl.ds(base, tall)] += added[:, 0:512]
        spill[pl.ds(base, tall)] += added[:, 512:640]

    @pl.when(led == pl.num_programs(0) - 1)
    def _():
        for tile in range(out.shape[0]):
            start = tile * 256
            out[tile, 0:256] = field[start : start + 256]
            both = spill[start : start + 128] + pltpu.roll(
                spill[start + 128 : start + 256], HALO, 1
            )
            for group in range(4):
                out[tile, 256:288, group * 128 : group * 128 + 128] = both[
                    group * 32 : group * 32 + 32
                ]


def residual_kernel(
    summed, spilled, modelled, out, below, above, to_left, to_right,
    left_below, left_above, right_below, right_above, square,
):
    tile = summed[0:256] - modelled[...]
    both = jnp.concatenate(
        [spilled[:, group * 128 : group * 128 + 128] for group in range(4)], axis=0
    )
    lane = lax.broadcasted_iota(jnp.int32, both.shape, 1)
    zero = jnp.zeros_like(both)

    def at_start(amount):
        return jnp.where(lane < HALO, pltpu.roll(both, amount, 1) if amount else both, zero)

    first = jnp.concatenate([at_start(0), at_start(96)], axis=0)
    second = jnp.concatenate([at_start(64), at_start(32)], axis=0)
    tile = jnp.concatenate(
        [tile[:, 0:128] + first, tile[:, 128:256], tile[:, 256:384] + second, tile[:, 384:512]],
        axis=1,
    )
    out[...] = tile
    below[...] = tile[256 - HALO :]
    above[...] = tile[:HALO]
    left = pack_edges(tile, True)
    right = pack_edges(tile, False)
    to_left[...] = left
    to_right[...] = right
    left_below[...] = left[256 - HALO :]
    left_above[...] = left[:HALO]
    right_below[...] = right[256 - HALO :]
    right_above[...] = right[:HALO]
    square[...] = jnp.broadcast_to(jnp.sum(tile * tile), square.shape)


def finish_kernel(step, own, residual, image_dir, out_spectrum, out_residual):
    size = step[0]
    for part in range(2):
        lanes = slice(part * 256, part * 256 + 256)
        direction = residual[:, lanes]
        out_spectrum[0, part] = own[0, part] + size * direction
        out_residual[0, part] = direction - size * image_dir[:, lanes]


def shape(*dims, dtype=F32):
    return jax.ShapeDtypeStruct(dims, dtype)


def grid_call(kernel, grid, prefetch, in_specs, out_specs, out_shape, scratch=(), cost=None):
    return pl.pallas_call(
        kernel,
        grid_spec=pltpu.PrefetchScalarGridSpec(
            num_scalar_prefetch=prefetch,
            grid=grid,
            in_specs=in_specs,
            out_specs=out_specs,
            scratch_shapes=scratch,
        ),
        out_shape=out_shape,
        compiler_params=pltpu.CompilerParams(vmem_limit_bytes=60 * 1024 * 1024),
        cost_estimate=cost,
    )


def fixed(*dims):
    return pl.BlockSpec(dims, lambda *_: (0,) * len(dims))


def per_led(*dims):
    return pl.BlockSpec((1, *dims), lambda led, *_: (led,) + (0,) * len(dims))


def body(spectrum, images, zernike, pupil_modes, patch_tiles, patch_offsets):
    tile_len = spectrum.shape[3]
    row_cells = spectrum.shape[2]
    strip_len = images.shape[2]
    image_len = images.shape[3]
    channel_count = zernike.shape[1]
    tap_count = pupil_modes.shape[2]
    reach = tap_count - 1
    spec_count = lax.axis_size("spec")
    led_count = lax.axis_size("led")
    leds = patch_tiles.shape[0]
    column_here = lax.axis_index("spec").astype(jnp.int32)
    strip_here = lax.axis_index("led").astype(jnp.int32)
    assert tile_len == 256 and row_cells == led_count * 256 and leds == spec_count
    assert tap_count <= HALO and strip_len == 128

    first_tiles = patch_tiles[:, 0]
    top_tiles = first_tiles // spec_count
    left_tiles = first_tiles % spec_count
    col_at = (column_here - left_tiles) * tile_len - patch_offsets[:, 1]
    row_at = (strip_here - top_tiles) * tile_len - patch_offsets[:, 0]
    starts = top_tiles * tile_len + patch_offsets[:, 0] + strip_here * strip_len
    own = jnp.stack([left_tiles, patch_offsets[:, 1]])[:, column_here]

    slots = grid_call(
        slots_kernel, (spec_count,), 1,
        [fixed(1, 2, strip_len, image_len)],
        per_led(2, strip_len, tile_len),
        shape(spec_count, 2, strip_len, tile_len),
        [pltpu.VMEM((2, strip_len, WIN * tile_len), F32)],
    )(own, images)
    pieces = lax.all_to_all(slots, "spec", split_axis=0, concat_axis=0, tiled=True)

    all_modes = lax.all_gather(pupil_modes, "led", axis=0, tiled=True)
    flat_modes = all_modes.reshape(channel_count, 4 * tap_count)
    own_kernel = jnp.dot(zernike, flat_modes, precision=lax.Precision.HIGHEST)
    own_kernel = jnp.pad(own_kernel.reshape(4, tap_count), ((0, 0), (0, HALO - tap_count)))
    kernels = lax.all_to_all(
        jnp.broadcast_to(own_kernel.reshape(1, 4 * HALO), (spec_count, 4 * HALO)),
        "spec", split_axis=0, concat_axis=0, tiled=True,
    ).reshape(leds, 4, HALO)[:, :, :tap_count]
    ahead = HALO - reach
    taps = jnp.concatenate(
        [
            jnp.pad(kernels, ((0, 0), (0, 0), (0, RING - tap_count))),
            jnp.pad(kernels[:, :, ::-1], ((0, 0), (0, 0), (ahead, RING - tap_count - ahead))),
        ],
        axis=1,
    )

    tall = 256 + 2 * HALO
    blocks = 256 // HALO
    last = led_count * blocks - 1
    where = jnp.stack([strip_here, jnp.int32(led_count - 1)])
    f_main, f_below, f_above, to_left, to_right = grid_call(
        cut_kernel, (1,), 1,
        [
            pl.BlockSpec((1, 2, 256, 256), lambda _, at: (0, 0, at[0], 0)),
            pl.BlockSpec(
                (1, 2, HALO, 256),
                lambda _, at: (0, 0, jnp.minimum(at[0] * blocks + blocks, last), 0),
            ),
            pl.BlockSpec(
                (1, 2, HALO, 256), lambda _, at: (0, 0, jnp.maximum(at[0] * blocks - 1, 0), 0)
            ),
        ],
        [fixed(256, 512), fixed(HALO, 512), fixed(HALO, 512), fixed(tall, 128), fixed(tall, 128)],
        [shape(256, 512), shape(HALO, 512), shape(HALO, 512), shape(tall, 128), shape(tall, 128)],
    )(where, spectrum, spectrum, spectrum)

    def hop(value, right, down):
        pairs = []
        for column in range(spec_count):
            for strip in range(led_count):
                to_column, to_strip = column + right, strip + down
                if 0 <= to_column < spec_count and 0 <= to_strip < led_count:
                    pairs.append((column * led_count + strip, to_column * led_count + to_strip))
        return lax.ppermute(value, ("spec", "led"), pairs)

    wide_left = [
        pltpu.VMEM((2 * tall, 640), BF16),
        pltpu.VMEM((2 * tall, 640), BF16),
    ]
    work = 2 * 1920 * 256 * (640 + 512) * 8
    modelled, col_high, col_low, row_high, row_low = grid_call(
        functools.partial(first_kernel, image_len, reach), (leds,), 2,
        [
            per_led(8, RING), fixed(256, 512), fixed(HALO, 512), fixed(HALO, 512),
            fixed(tall, 128), fixed(tall, 128),
        ],
        [fixed(256, 512), per_led(640, 256), per_led(640, 256), per_led(256, 640), per_led(256, 640)],
        [
            shape(256, 512), shape(leds, 640, 256, dtype=BF16), shape(leds, 640, 256, dtype=BF16),
            shape(leds, 256, 640, dtype=BF16), shape(leds, 256, 640, dtype=BF16),
        ],
        wide_left,
        pl.CostEstimate(flops=2 * work, bytes_accessed=22 << 20, transcendentals=0),
    )(col_at, row_at, taps, f_main, f_below, f_above, hop(to_right, 1, 0), hop(to_left, -1, 0))

    gathered = grid_call(
        functools.partial(data_kernel, image_len, reach), (leds,), 2,
        [per_led(8, RING), per_led(2, strip_len, 256)],
        fixed(led_count, 288, 512),
        shape(led_count, 288, 512),
        [pltpu.VMEM((row_cells + 16, 512), F32), pltpu.VMEM((row_cells + 16, 128), F32)],
        pl.CostEstimate(flops=work // 2, bytes_accessed=9 << 20, transcendentals=0),
    )(col_at, starts, taps, pieces)
    summed = lax.psum_scatter(gathered, "led", scatter_dimension=0, tiled=True)[0]
    spilled = hop(summed[256:288], 1, 0)

    edge = [shape(HALO, 512)] * 2 + [shape(256, 128)] * 2 + [shape(HALO, 128)] * 4
    (
        residual, below, above, to_left, to_right,
        left_below, left_above, right_below, right_above, square,
    ) = pl.pallas_call(
        residual_kernel,
        out_shape=[shape(256, 512), *edge, shape(8, 128)],
    )(summed, spilled, modelled)
    all_residual = lax.all_gather(residual, "led", axis=0, tiled=True)

    image_dir, inner = grid_call(
        functools.partial(second_kernel, image_len, reach), (leds,), 2,
        [per_led(640, 256), per_led(640, 256), per_led(256, 640), per_led(256, 640),
         fixed(256, 512), fixed(HALO, 512), fixed(HALO, 512), fixed(256, 128), fixed(256, 128),
         *[fixed(HALO, 128)] * 4],
        [fixed(256, 512), fixed(8, 128)],
        [shape(256, 512), shape(8, 128)],
        wide_left,
        pl.CostEstimate(flops=work, bytes_accessed=22 << 20, transcendentals=0),
    )(
        col_at, row_at, col_high, col_low, row_high, row_low,
        residual, hop(above, 0, -1), hop(below, 0, 1), hop(to_right, 1, 0), hop(to_left, -1, 0),
        hop(right_above, 1, -1), hop(left_above, -1, -1),
        hop(right_below, 1, 1), hop(left_below, -1, 1),
    )
    all_image_dir = lax.all_gather(image_dir, "led", axis=0, tiled=True)

    lane = lax.broadcasted_iota(jnp.int32, (1, 128), 1)
    sums = jnp.where(lane == 0, square[0:1], inner[0:1])
    sums = jnp.sum(lax.all_gather(sums, "led", axis=0, tiled=True), axis=0, keepdims=True)
    sums = lax.all_to_all(
        jnp.broadcast_to(sums, (spec_count, 128)), "spec", split_axis=0, concat_axis=0, tiled=True
    )
    sums = jnp.sum(sums, axis=0)
    step = (sums[0] / sums[1]).reshape(1)

    return grid_call(
        finish_kernel, (led_count,), 1,
        [
            pl.BlockSpec((1, 2, 256, 256), lambda row, _: (0, 0, row, 0)),
            pl.BlockSpec((256, 512), lambda row, _: (row, 0)),
            pl.BlockSpec((256, 512), lambda row, _: (row, 0)),
        ],
        [pl.BlockSpec((1, 2, 256, 256), lambda row, _: (0, 0, row, 0))] * 2,
        [shape(1, 2, row_cells, 256)] * 2,
    )(step, spectrum, all_residual, all_image_dir)


def solution(mesh):
    placed = (
        P("spec", None, None, None),
        P("spec", None, "led", None),
        P("spec", None),
        P("led", None, None),
        P(),
        P(),
    )
    return jax.shard_map(
        body,
        mesh=mesh,
        in_specs=placed,
        out_specs=(P("spec", None, None, None), P("spec", None, None, None)),
        check_vma=False,
    )
```
